256 devices in a mesh: dp: 8 (over z), seq: 32 (over y, x, core).
Axes of the slice: x: 4, y: 4, z: 8, core: 2. Of those that a mesh axis runs over, the one named last changes fastest.
Arguments:
- embeddings: bfloat16 [8, 4096, 1536], P('dp', 'seq'), may hold values from -6 to 6
- conv_one: bfloat16 [3, 1536, 1536], P(None, 'dp'), may hold values from -0.09375 to 0.09375
- conv_two: bfloat16 [3, 1536, 1536], P(None, 'dp'), may hold values from -0.09375 to 0.09375
- head_weight: bfloat16 [1536, 3072], P(None, 'dp'), may hold values from -4 to 4
- counts: int32 [8, 4096, 3072], P(None, 'seq', 'dp'), may hold values from 0 to 12
- dilation: int32 [2], replicated, may hold values from 1 to 32, as said below
Outputs:
- track_loss: float32 [8, 3072], P(None, 'dp')
- grad_head: float32 [1536, 3072], P('seq', 'dp')
- grad_one: float32 [3, 1536, 1536], P(None, 'seq', 'dp')
- grad_two: float32 [3, 1536, 1536], P(None, 'seq', 'dp')
The draws below stay inside these ranges and needn't reach their ends.
Inputs may be any that keep to these rules, and one draw needn't show every extreme that they name: One of the two convolutions has dilation 32, the other a smaller one.
All inputs are finite; a program needn't handle non-finite values.
Results may differ from the reference program's by a relative error of at most 0.019.
The reference program's roundings to bfloat16 on the way count: a program that leaves them out, or rounds other values in their place, can miss the bound.
Values may be sent and summed in bfloat16 or wider, within the bound.
A program may use at most 128 MiB of HBM per device.

```python
import math
import jax
import jax.numpy as jnp
from jax import lax

C = 1536
TR = 3072
DMAX = 32
BATCH = 8
BINS = 4096
N_DP = 8


def draw_head_weight(key, part):
    normal_part = jax.random.normal(key, (C, TR), jnp.float32) / math.sqrt(C)
    return normal_part.astype(jnp.bfloat16)


def draw_counts(key, part):
    position = jnp.arange(BINS, dtype=jnp.int32)
    ceiling = 4 + 9 * position // BINS
    return jax.random.randint(key, (BATCH, BINS, TR), 0, ceiling[None, :, None] + 1, dtype=jnp.int32)


def draw_dilation(key, part):
    second = jax.random.randint(jax.random.fold_in(key, 1), (), 1, DMAX, dtype=jnp.int32)
    chosen_slot = jax.random.randint(jax.random.fold_in(key, 2), (), 0, 2, dtype=jnp.int32)
    return jnp.where(jnp.arange(2, dtype=jnp.int32) == chosen_slot, DMAX, second).astype(jnp.int32)


def levels(key, extent, split, least, largest):
    def one(dim, parts):
        steps = jax.random.uniform(jax.random.fold_in(jax.random.fold_in(key, 6), dim), (parts,), jnp.float32, least / len(split), largest / len(split))
        return jnp.repeat(jnp.exp(steps), extent[dim] // parts).reshape((-1,) + (1,) * (len(extent) - dim - 1))

    gain = one(*split[0])
    for cut in split[1:]:
        gain = gain * one(*cut)
    return gain


def noise(rng, shape, spread, bound, pieces=(), kind=jnp.bfloat16):
    array = spread * jax.random.normal(rng, shape, jnp.float32)
    if pieces:
        array = array * levels(rng, shape, pieces, -0.22, 0.18)
    return jnp.clip(array, -bound, bound).astype(kind)


def setup_inputs(seed: int = 0) -> dict:
    seeds = jax.random.split(jax.random.key(seed), 7)
    return {
        "embeddings": noise(seeds[0], (BATCH, BINS, C), 1.0, 6.0, ((0, 8), (1, 32))),
        "conv_one": noise(seeds[1], (3, C, C), (3 * C) ** -0.5, 0.09375, ((1, 8),)),
        "conv_two": noise(seeds[2], (3, C, C), (3 * C) ** -0.5, 0.09375, ((1, 8),)),
        "head_weight": draw_head_weight(jax.random.fold_in(seeds[6], 71), 0),
        "counts": draw_counts(jax.random.fold_in(seeds[6], 71), 0),
        "dilation": draw_dilation(jax.random.fold_in(seeds[6], 71), 0),
    }


def activate(value):
    return jax.nn.gelu(value)

def padded_rows(field):
    return jnp.pad(field, ((DMAX, DMAX), (0, 0)))

def shifted_rows(padded, spacing, sign, tap_index):
    return lax.dynamic_slice_in_dim(padded, (DMAX + sign * (tap_index - 1) * spacing).astype(jnp.int32), BINS, 0)

def conv_forward(padded, weight, spacing):
    running = jnp.zeros((BINS, weight.shape[1]), jnp.float32)
    for tap_index in range(3):
        running = running + jnp.dot(shifted_rows(padded, spacing, 1, tap_index), weight[tap_index].T, preferred_element_type=jnp.float32)
    return running

def conv_weight_grad(padded, upstream, spacing):
    grads = []
    for tap_index in range(3):
        grads.append(jnp.dot(shifted_rows(padded, spacing, 1, tap_index).T, upstream, preferred_element_type=jnp.float32))
    return jnp.stack(grads)

def conv_input_grad(upstream, weight, spacing):
    padded = padded_rows(upstream)
    width = C // N_DP
    running = jnp.zeros((BINS, C), jnp.float32)
    for group_index in range(N_DP):
        partial_sum = jnp.zeros((BINS, C), jnp.float32)
        for tap_index in range(3):
            shifted = shifted_rows(padded, spacing, -1, tap_index)[:, group_index * width:(group_index + 1) * width]
            block_weight = weight[tap_index][group_index * width:(group_index + 1) * width, :]
            partial_sum = partial_sum + jnp.dot(shifted, block_weight, preferred_element_type=jnp.float32)
        rounded = lax.optimization_barrier(partial_sum.astype(jnp.bfloat16))
        running = running + rounded.astype(jnp.float32)
    return running

def head_input_grad(logit_grad, head_weight):
    width = TR // N_DP
    running = jnp.zeros((BINS, C), jnp.float32)
    for group_index in range(N_DP):
        partial_sum = jnp.dot(logit_grad[:, group_index * width:(group_index + 1) * width], head_weight[:, group_index * width:(group_index + 1) * width].T, preferred_element_type=jnp.float32)
        rounded = lax.optimization_barrier(partial_sum.astype(jnp.bfloat16))
        running = running + rounded.astype(jnp.float32)
    return running

def reference(embeddings, conv_one, conv_two, head_weight, counts, dilation):
    first_gap = dilation[0]
    second_gap = dilation[1]

    def one_sequence(inputs_one):
        field, count_rows = inputs_one
        targets = count_rows.astype(jnp.float32)
        framed_in = padded_rows(field)
        pre_one = conv_forward(framed_in, conv_one, first_gap)
        hidden_one = (field.astype(jnp.float32) + activate(pre_one)).astype(jnp.bfloat16)
        framed_one = padded_rows(hidden_one)
        pre_two = conv_forward(framed_one, conv_two, second_gap)
        hidden_two = (hidden_one.astype(jnp.float32) + activate(pre_two)).astype(jnp.bfloat16)
        logits = jnp.dot(hidden_two, head_weight, preferred_element_type=jnp.float32)
        peak_all = lax.optimization_barrier(jnp.max(logits, axis=0))
        exp_total = lax.optimization_barrier(jnp.sum(jnp.exp(logits - peak_all[None, :]), axis=0))
        log_total = peak_all + jnp.log(exp_total)
        count_total = lax.optimization_barrier(jnp.sum(targets, axis=0))
        cross_total = lax.optimization_barrier(jnp.sum(targets * logits, axis=0))
        track_loss = (count_total * log_total - cross_total) / BINS
        logit_grad = ((count_total[None, :] * jnp.exp(logits - log_total[None, :]) - targets) / BINS).astype(jnp.bfloat16)
        grad_head = jnp.dot(hidden_two.T, logit_grad, preferred_element_type=jnp.float32)
        grad_two_out = head_input_grad(logit_grad, head_weight)
        upstream_two = jax.vjp(activate, pre_two)[1](grad_two_out)[0].astype(jnp.bfloat16)
        grad_two = conv_weight_grad(framed_one, upstream_two, second_gap)
        grad_one_out = grad_two_out + conv_input_grad(upstream_two, conv_two, second_gap)
        upstream_one = jax.vjp(activate, pre_one)[1](grad_one_out)[0].astype(jnp.bfloat16)
        grad_one = conv_weight_grad(framed_in, upstream_one, first_gap)
        return (track_loss, grad_head, grad_one, grad_two)
    losses, heads, ones, twos = lax.map(one_sequence, (embeddings, counts))
    return (losses, lax.optimization_barrier(jnp.sum(heads, axis=0)), lax.optimization_barrier(jnp.sum(ones, axis=0)), lax.optimization_barrier(jnp.sum(twos, axis=0)))
```

```python
import functools

import jax
import jax.numpy as jnp
from jax import lax
from jax.experimental import pallas as pl
from jax.experimental.pallas import tpu as pltpu
from jax.sharding import PartitionSpec as P

DMAX = 32
NZ = 8
MESH = pl.DeviceIdType.MESH
BF = jnp.bfloat16
F32 = jnp.float32


def remote(src, dst, send, recv, device):
    return pltpu.make_async_remote_copy(
        src_ref=src, dst_ref=dst, send_sem=send, recv_sem=recv, device_id=device, device_id_type=MESH
    )


def greet(devices):
    barrier = pltpu.get_barrier_semaphore()
    for device in devices:
        pl.semaphore_signal(barrier, inc=1, device_id=device, device_id_type=MESH)
    pl.semaphore_wait(barrier, len(devices))


def z_neighbours():
    z = lax.axis_index("dp")
    return z, lax.rem(z + 1, NZ), lax.rem(z + NZ - 1, NZ)


def seq_neighbours():
    s, n = lax.axis_index("seq"), lax.axis_size("seq")
    return s, lax.rem(s + 1, n), lax.rem(s + n - 1, n)


def ring_gather(own, slot, half_rows, send_sem, recv_sem, on_block):
    z, right, left = z_neighbours()
    copies = {}
    for way in (0, 1):
        sign = -1 if way == 0 else 1
        peer = {"dp": right if way == 0 else left}
        for step in range(4):
            block = lax.rem(z + sign * step + NZ, NZ)
            for half in (0, 1):
                if step == 3 and half != way:
                    continue
                source = own(half) if step == 0 else slot(block, half)
                copies[way, step, half] = remote(
                    source, slot(block, half), send_sem.at[way, step, half], recv_sem.at[way, step, half], peer
                )
    for half in (0, 1):
        for way in (0, 1):
            copies[way, 0, half].start()
    on_block(0, z)
    for step in (1, 2, 3):
        for half in (0, 1):
            for way in (0, 1):
                copies[way, step - 1, half].wait_recv()
                if (way, step, half) in copies:
                    copies[way, step, half].start()
        on_block(2 * step - 1, lax.rem(z - step + NZ, NZ))
        on_block(2 * step, lax.rem(z + step, NZ))
    copies[0, 3, 0].wait_recv()
    copies[1, 3, 1].wait_recv()
    on_block(7, lax.rem(z + 4, NZ))
    for copy in copies.values():
        copy.wait_send()


def rows_gather_kernel(x_ref, out_ref, send_sem, recv_sem, edge_send, edge_recv, own_sem):
    length = x_ref.shape[0]
    z, right, left = z_neighbours()
    s, after, before = seq_neighbours()
    greet([{"dp": right}, {"dp": left}, {"seq": after}, {"seq": before}])
    mine = pltpu.make_async_copy(x_ref, out_ref.at[z, pl.ds(DMAX, length)], own_sem)
    mine.start()
    half_rows = length // 2
    edges = []

    def on_block(order, block):
        if order == 0:
            first, last = x_ref.at[pl.ds(0, DMAX)], x_ref.at[pl.ds(length - DMAX, DMAX)]
        else:
            first, last = out_ref.at[block, pl.ds(DMAX, DMAX)], out_ref.at[block, pl.ds(length, DMAX)]
        for side, (src, dst, peer) in enumerate(
            (
                (last, out_ref.at[block, pl.ds(0, DMAX)], after),
                (first, out_ref.at[block, pl.ds(DMAX + length, DMAX)], before),
            )
        ):
            copy = remote(src, dst, edge_send.at[side, order], edge_recv.at[side, order], {"seq": peer})
            copy.start()
            edges.append(copy)

    ring_gather(
        lambda h: x_ref.at[pl.ds(h * half_rows, half_rows)],
        lambda k, h: out_ref.at[k, pl.ds(DMAX + h * half_rows, half_rows)],
        half_rows,
        send_sem,
        recv_sem,
        on_block,
    )
    for copy in edges:
        copy.wait_recv()
        copy.wait_send()
    mine.wait()

    @pl.when(s == 0)
    def _():
        out_ref[:, 0:DMAX, :] = jnp.zeros_like(out_ref[:, 0:DMAX, :])

    @pl.when(s == lax.axis_size("seq") - 1)
    def _():
        out_ref[:, length + DMAX :, :] = jnp.zeros_like(out_ref[:, length + DMAX :, :])


def whole(n):
    return [pl.BlockSpec(memory_space=pltpu.VMEM)] * n


def rows_gather(x, collective_id):
    length, width = x.shape
    return pl.pallas_call(
        rows_gather_kernel,
        out_shape=jax.ShapeDtypeStruct((NZ, length + 2 * DMAX, width), x.dtype),
        in_specs=whole(1),
        out_specs=whole(1)[0],
        scratch_shapes=[
            pltpu.SemaphoreType.DMA((2, 4, 2)),
            pltpu.SemaphoreType.DMA((2, 4, 2)),
            pltpu.SemaphoreType.DMA((2, 8)),
            pltpu.SemaphoreType.DMA((2, 8)),
            pltpu.SemaphoreType.DMA,
        ],
        compiler_params=pltpu.CompilerParams(collective_id=collective_id, has_side_effects=True),
        name="rows_gather",
    )(x)


LO, HI = slice(0, 64), slice(64, 128)


def chan_gather_kernel(framed, x_ref, out_ref, held, edge, send_sem, recv_sem, edge_send, edge_recv):
    rows = x_ref.shape[0]
    part = rows // 2
    rim = 8 * DMAX
    base = rim if framed else 0
    z, right, left = z_neighbours()
    s, after, before = seq_neighbours()
    held[z, 0:rows, :] = x_ref[:, 0:128]
    held[z, rows : rows + part, :] = jnp.concatenate([x_ref[0:part, 128:192], x_ref[part:rows, 128:192]], axis=1)
    peers = [{"dp": right}, {"dp": left}]
    if framed:
        peers += [{"seq": after}, {"seq": before}]
    greet(peers)
    half_rows = (rows + part) // 2
    edges = []

    def on_block(order, block):
        if not framed:
            return
        for side, piece, start, peer in (
            (0, 0, rows - rim, after),
            (0, 1, rows + part - rim, after),
            (1, 0, 0, before),
            (1, 1, rows, before),
        ):
            copy = remote(
                held.at[block, pl.ds(start, rim)],
                edge.at[side, block, pl.ds(piece * rim, rim)],
                edge_send.at[side, piece, order],
                edge_recv.at[side, piece, order],
                {"seq": peer},
            )
            copy.start()
            edges.append(copy)

    ring_gather(
        lambda h: held.at[z, pl.ds(h * half_rows, half_rows)],
        lambda k, h: held.at[k, pl.ds(h * half_rows, half_rows)],
        half_rows,
        send_sem,
        recv_sem,
        on_block,
    )
    for j in range(NZ // 2):
        one, two, lane = 2 * j, 2 * j + 1, 384 * j
        out_ref[base : base + rows, lane : lane + 128] = held[one, 0:rows, :]
        out_ref[base : base + rows, lane + 256 : lane + 384] = held[two, 0:rows, :]
        for h, lanes in ((0, LO), (1, HI)):
            out_ref[base + h * part : base + (h + 1) * part, lane + 128 : lane + 256] = jnp.concatenate(
                [held[one, rows : rows + part, lanes], held[two, rows : rows + part, lanes]], axis=1
            )
    if framed:
        for copy in edges:
            copy.wait_recv()
            copy.wait_send()
        n = lax.axis_size("seq")
        for side, at, lanes, keep in ((0, 0, HI, s > 0), (1, base + rows, LO, s < n - 1)):
            for j in range(NZ // 2):
                one, two, lane = 2 * j, 2 * j + 1, 384 * j
                pieces = (
                    edge[side, one, 0:rim, :],
                    jnp.concatenate([edge[side, one, rim : 2 * rim, lanes], edge[side, two, rim : 2 * rim, lanes]], axis=1),
                    edge[side, two, 0:rim, :],
                )
                for i, piece in enumerate(pieces):
                    out_ref[at : at + rim, lane + 128 * i : lane + 128 * (i + 1)] = jnp.where(
                        keep, piece, jnp.zeros_like(piece)
                    )


def chan_gather(x, framed, collective_id):
    rows = x.shape[0]
    rim = 8 * DMAX
    return pl.pallas_call(
        functools.partial(chan_gather_kernel, framed),
        out_shape=jax.ShapeDtypeStruct((rows + (2 * rim if framed else 0), 192 * NZ), x.dtype),
        in_specs=whole(1),
        out_specs=whole(1)[0],
        scratch_shapes=[
            pltpu.VMEM((NZ, rows + rows // 2, 128), x.dtype),
            pltpu.VMEM((2, NZ, 2 * rim, 128) if framed else (1, 1, 16, 128), x.dtype),
            pltpu.SemaphoreType.DMA((2, 4, 2)),
            pltpu.SemaphoreType.DMA((2, 4, 2)),
            pltpu.SemaphoreType.DMA((2, 2, 8)),
            pltpu.SemaphoreType.DMA((2, 2, 8)),
        ],
        compiler_params=pltpu.CompilerParams(collective_id=collective_id, has_side_effects=True),
        name="chan_gather",
    )(x)


def chan_scatter_kernel(p_ref, out_ref, own, got, sent, send_sem, recv_sem):
    rows = p_ref.shape[0]
    part = rows // 2
    half_rows = (rows + part) // 2
    z, right, left = z_neighbours()
    for j in range(NZ // 2):
        one, two, lane = 2 * j, 2 * j + 1, 384 * j
        own[one, 0:rows, :] = p_ref[:, lane : lane + 128]
        own[two, 0:rows, :] = p_ref[:, lane + 256 : lane + 384]
        for block, lanes in ((one, slice(lane + 128, lane + 192)), (two, slice(lane + 192, lane + 256))):
            own[block, rows : rows + part, :] = jnp.concatenate([p_ref[0:part, lanes], p_ref[part:rows, lanes]], axis=1)
    greet([{"dp": right}, {"dp": left}])
    piece = lambda h: pl.ds(h * half_rows, half_rows)
    copies = {}
    for step in range(4):
        for half in (0, 1):
            for way in (0, 1):
                if step == 0 and half != way:
                    continue
                sign = 1 if way == 0 else -1
                block = lax.rem(z + sign * (4 - step) + NZ, NZ)
                before = copies.get((way, step - 1, half))
                if before is None:
                    source = own.at[block, piece(half)]
                else:
                    before.wait_recv()
                    sent[way, step - 1, piece(half), :] = (
                        got[way, step - 1, piece(half), :].astype(F32) + own[block, piece(half), :].astype(F32)
                    ).astype(BF)
                    source = sent.at[way, step - 1, piece(half)]
                copy = remote(
                    source,
                    got.at[way, step, piece(half)],
                    send_sem.at[way, step, half],
                    recv_sem.at[way, step, half],
                    {"dp": right if way == 0 else left},
                )
                copy.start()
                copies[way, step, half] = copy
    for half in (0, 1):
        copies[0, 3, half].wait_recv()
        copies[1, 3, half].wait_recv()

    def total(at, size):
        return (
            own[z, at : at + size, :].astype(F32)
            + got[0, 3, at : at + size, :].astype(F32)
            + got[1, 3, at : at + size, :].astype(F32)
        )

    out_ref[:, 0:128] = total(0, rows)
    rest = total(rows, part)
    out_ref[0:part, 128:192] = rest[:, LO]
    out_ref[part:rows, 128:192] = rest[:, HI]
    for copy in copies.values():
        copy.wait_send()


def chan_scatter(partial, collective_id):
    rows = partial.shape[0]
    block = (rows + rows // 2, 128)
    return pl.pallas_call(
        chan_scatter_kernel,
        out_shape=jax.ShapeDtypeStruct((rows, 192), F32),
        in_specs=whole(1),
        out_specs=whole(1)[0],
        scratch_shapes=[
            pltpu.VMEM((NZ, *block), BF),
            pltpu.VMEM((2, 4, *block), BF),
            pltpu.VMEM((2, 3, *block), BF),
            pltpu.SemaphoreType.DMA((2, 4, 2)),
            pltpu.SemaphoreType.DMA((2, 4, 2)),
        ],
        compiler_params=pltpu.CompilerParams(collective_id=collective_id, has_side_effects=True),
        name="chan_scatter",
    )(partial)


def seq_place():
    s = lax.axis_index("seq")
    return s // 8, lax.rem(s // 2, 4), lax.rem(s, 2)


def seq_peers():
    y, x, core = seq_place()
    at = lambda y, x, core: (y * 4 + x) * 2 + core
    other = at(y, x, 1 - core)
    along_x = [at(y, lax.rem(x + d, 4), core) for d in (1, 2, 3)]
    along_y = [at(lax.rem(y + d, 4), x, core) for d in (1, 2, 3)]
    return other, along_x, along_y


def stats_kernel(x_ref, out_ref, merged, got, send_sem, recv_sem, own_sem):
    y, x, core = seq_place()
    other, along_x, along_y = seq_peers()
    greet([{"seq": p} for p in [other, *along_x, *along_y]])
    stages = ((2, core, [other]), (4, x, along_x), (4, y, along_y))
    base = 0
    for number, (count, place, peers) in enumerate(stages):
        source = x_ref if number == 0 else merged.at[number - 1]
        copies = []
        for d, peer in enumerate(peers):
            copy = remote(
                source,
                got.at[number, place],
                send_sem.at[number, d],
                recv_sem.at[number, d],
                {"seq": peer},
            )
            copy.start()
            copies.append(copy)
        mine = pltpu.make_async_copy(source, got.at[number, place], own_sem.at[number])
        mine.start()
        mine.wait()
        for copy in copies:
            copy.wait_recv()
        peak = got[number, 0, 0]
        for i in range(1, count):
            peak = jnp.maximum(peak, got[number, i, 0])
        sums = [jnp.zeros_like(peak) for _ in range(3)]
        for i in range(count):
            sums[0] = sums[0] + got[number, i, 1] * jnp.exp(got[number, i, 0] - peak)
            sums[1] = sums[1] + got[number, i, 2]
            sums[2] = sums[2] + got[number, i, 3]
        for copy in copies:
            copy.wait_send()
        target = out_ref if number == 2 else merged.at[number]
        target[0] = peak
        for i in range(3):
            target[i + 1] = sums[i]


def merge_stats(stats, collective_id):
    shape = stats.shape
    return pl.pallas_call(
        stats_kernel,
        out_shape=jax.ShapeDtypeStruct(shape, F32),
        in_specs=whole(1),
        out_specs=whole(1)[0],
        scratch_shapes=[
            pltpu.VMEM((2, *shape), F32),
            pltpu.VMEM((3, 4, *shape), F32),
            pltpu.SemaphoreType.DMA((3, 3)),
            pltpu.SemaphoreType.DMA((3, 3)),
            pltpu.SemaphoreType.DMA((3,)),
        ],
        compiler_params=pltpu.CompilerParams(collective_id=collective_id, has_side_effects=True),
        name="merge_stats",
    )(stats)


def seq_scatter_kernel(
    x_ref, out_ref, pair, both, got_one, mid_one, got_two, sems_send, sems_recv, pair_send, pair_recv
):
    y, x, core = seq_place()
    other, along_x, along_y = seq_peers()
    rows = x_ref.shape[2]
    half = rows // 2
    greet([{"seq": p} for p in [other, *along_x, *along_y]])
    pairs = []
    for h in (0, 1):
        for q in range(4):
            copy = remote(
                x_ref.at[1 - core, pl.ds(4 * q, 4), pl.ds(h * half, half)],
                pair.at[h, pl.ds(4 * q, 4)],
                pair_send.at[h, q],
                pair_recv.at[h, q],
                {"seq": other},
            )
            copy.start()
            pairs.append(copy)
    copies = {}
    for h in (0, 1):
        for q in range(4):
            pairs[4 * h + q].wait_recv()

            @pl.loop(4 * q, 4 * q + 4)
            def _(i):
                total = pair[h, i].astype(F32) + x_ref[core, i, pl.ds(h * half, half), :].astype(F32)
                spot = lax.rem(i, 4) * 4 + i // 4 if h == 0 else i
                both[h, spot] = total.astype(BF)

        place, peers = (x, along_x) if h == 0 else (y, along_y)
        for d, peer in enumerate(peers):
            target = lax.rem(place + d + 1, 4)
            copy = remote(
                both.at[h, pl.ds(4 * target, 4)],
                got_one.at[h, 2 - d],
                sems_send.at[h, 0, d],
                sems_recv.at[h, 0, d],
                {"seq": peer},
            )
            copy.start()
            copies[h, 0, d] = copy
    for h in (0, 1):
        place = x if h == 0 else y
        for d in range(3):
            copies[h, 0, d].wait_recv()

        @pl.loop(0, 4)
        def _(i):
            total = both[h, 4 * place + i].astype(F32)
            for d in range(3):
                total = total + got_one[h, d, i].astype(F32)
            mid_one[h, i] = total.astype(BF)

        place, peers = (y, along_y) if h == 0 else (x, along_x)
        for d, peer in enumerate(peers):
            target = lax.rem(place + d + 1, 4)
            copy = remote(
                mid_one.at[h, target],
                got_two.at[h, 2 - d],
                sems_send.at[h, 1, d],
                sems_recv.at[h, 1, d],
                {"seq": peer},
            )
            copy.start()
            copies[h, 1, d] = copy
    for h in (0, 1):
        place = y if h == 0 else x
        for d in range(3):
            copies[h, 1, d].wait_recv()
        total = mid_one[h, place].astype(F32)
        for d in range(3):
            total = total + got_two[h, d].astype(F32)
        out_ref[h * half : (h + 1) * half, :] = total
    for copy in pairs:
        copy.wait_send()
    for copy in copies.values():
        copy.wait_send()


def seq_scatter(packed, collective_id):
    rows = packed.shape[2]
    half = rows // 2
    return pl.pallas_call(
        seq_scatter_kernel,
        out_shape=jax.ShapeDtypeStruct((rows, 128), F32),
        in_specs=whole(1),
        out_specs=whole(1)[0],
        scratch_shapes=[
            pltpu.VMEM((2, 16, half, 128), BF),
            pltpu.VMEM((2, 16, half, 128), BF),
            pltpu.VMEM((2, 3, 4, half, 128), BF),
            pltpu.VMEM((2, 4, half, 128), BF),
            pltpu.VMEM((2, 3, half, 128), BF),
            pltpu.SemaphoreType.DMA((2, 2, 3)),
            pltpu.SemaphoreType.DMA((2, 2, 3)),
            pltpu.SemaphoreType.DMA((2, 4)),
            pltpu.SemaphoreType.DMA((2, 4)),
        ],
        compiler_params=pltpu.CompilerParams(collective_id=collective_id, has_side_effects=True),
        name="seq_scatter",
    )(packed)


def activate(value):
    return jax.nn.gelu(value)


def shifted_taps(padded, spacing, length, sign):
    return [
        lax.dynamic_slice_in_dim(padded, DMAX + sign * (tap_index - 1) * spacing, length, 0) for tap_index in range(3)
    ]


def conv_apply(padded, weight, spacing, length):
    running = None
    for tap_index, rows in enumerate(shifted_taps(padded, spacing, length, 1)):
        term = jnp.einsum(
            "lc,dc->ld", rows.reshape(-1, rows.shape[2]), weight[tap_index], preferred_element_type=F32
        )
        running = term if running is None else running + term
    return running


def weight_grad(padded, upstream, spacing, length):
    return jnp.stack(
        [
            jnp.einsum("lc,ld->cd", rows.reshape(-1, rows.shape[2]), upstream, preferred_element_type=F32)
            for rows in shifted_taps(padded, spacing, length, 1)
        ]
    )


def seq_halo(value, width):
    size, length = lax.axis_size("seq"), value.shape[0]
    up = [(i, i + 1) for i in range(size - 1)]
    down = [(j, i) for i, j in up]
    before = lax.ppermute(value[length - width :], "seq", up)
    after = lax.ppermute(value[:width], "seq", down)
    return jnp.concatenate([before, value, after], axis=0)


def pack_head(grad):
    return grad.reshape(32, 48, 3, 128).transpose(0, 2, 1, 3).reshape(32, 144, 128).astype(BF)


def pack_conv(grad):
    blocks = grad.astype(BF).reshape(3, 32, 48, 192).transpose(1, 0, 2, 3).reshape(32, 144, 192)
    rest = jnp.concatenate([blocks[:, 0:72, 128:], blocks[:, 72:, 128:]], axis=2)
    return jnp.concatenate([blocks[:, :, :128], rest], axis=1)


def unpack_conv(block, odd):
    rest = jnp.concatenate([block[144:, 0:64], block[144:, 64:]], axis=0)
    main = block[:144]
    even_form = jnp.concatenate([main, rest], axis=1)
    odd_form = jnp.concatenate([rest, main], axis=1)
    return jnp.where(odd, odd_form, even_form).reshape(3, 48, 192)


def on_device(embeddings, conv_one, conv_two, head_weight, counts, dilation):
    length = embeddings.shape[1]
    chan_dev = conv_one.shape[1]
    own_index = lax.axis_index("dp")
    odd = lax.rem(own_index, 2) == 1
    turn = lambda w: jnp.where(odd, jnp.concatenate([w[:, 64:], w[:, :64]], axis=1), w)
    w_one, w_two = turn(conv_one), turn(conv_two)
    first_gap, second_gap = dilation[0], dilation[1]
    framed_in = jnp.transpose(rows_gather(embeddings[0], 0), (1, 0, 2))
    pre_one = conv_apply(framed_in, w_one, first_gap, length)
    centre_in = lax.slice_in_dim(framed_in, DMAX, DMAX + length, axis=0).reshape(-1, framed_in.shape[2])
    own_in = lax.dynamic_slice_in_dim(centre_in, own_index * chan_dev, chan_dev, 1)
    own_in = jnp.where(odd, jnp.concatenate([own_in[:, 64:], own_in[:, :64]], axis=1), own_in)
    hidden_one = (own_in.astype(F32) + activate(pre_one)).astype(BF)
    framed_one = chan_gather(hidden_one, True, 1).reshape(length + 2 * DMAX, NZ, -1)
    pre_two = conv_apply(framed_one, w_two, second_gap, length)
    hidden_two = (hidden_one.astype(F32) + activate(pre_two)).astype(BF)
    head_rows = chan_gather(hidden_two, False, 2)
    logits = jnp.einsum("lc,ct->lt", head_rows, head_weight, preferred_element_type=F32)
    logits = logits.reshape(length, NZ, -1)
    targets = jnp.transpose(counts, (1, 0, 2)).astype(F32)
    local_peak = jnp.max(logits, axis=0)
    stats = jnp.stack(
        [
            local_peak,
            jnp.sum(jnp.exp(logits - local_peak[None]), axis=0),
            jnp.sum(targets, axis=0),
            jnp.sum(targets * logits, axis=0),
        ]
    )
    peak_all, exp_total, count_total, cross_total = merge_stats(stats, 3)
    all_bins = length * lax.axis_size("seq")
    log_total = peak_all + jnp.log(exp_total)
    track_loss = (count_total * log_total - cross_total) / all_bins
    logit_grad = ((count_total[None] * jnp.exp(logits - log_total[None]) - targets) / all_bins).astype(BF)
    logit_grad = logit_grad.reshape(length * NZ, -1)
    grad_head = jnp.einsum("lc,lt->ct", head_rows, logit_grad, preferred_element_type=F32)
    back_partial = jnp.einsum("lt,ct->lc", logit_grad, head_weight, preferred_element_type=F32).astype(BF)
    grad_two_out = chan_scatter(back_partial, 4)
    upstream_two = jax.vjp(activate, pre_two)[1](grad_two_out)[0].astype(BF)
    grad_two = weight_grad(framed_one, upstream_two, second_gap, length)
    framed_back = seq_halo(upstream_two.reshape(length, NZ, -1), DMAX)
    conv_partial = None
    for tap_index, rows in enumerate(shifted_taps(framed_back, second_gap, length, -1)):
        term = jnp.einsum("ld,dc->lc", rows.reshape(length * NZ, -1), w_two[tap_index], preferred_element_type=F32)
        conv_partial = term if conv_partial is None else conv_partial + term
    grad_one_out = grad_two_out + chan_scatter(conv_partial.astype(BF), 5)
    upstream_one = jax.vjp(activate, pre_one)[1](grad_one_out)[0].astype(BF)
    grad_one = weight_grad(framed_in, upstream_one, first_gap, length)
    packed = jnp.concatenate([pack_head(grad_head), pack_conv(grad_two), pack_conv(grad_one)], axis=1)
    packed = packed.reshape(16, 2, 576, 128).transpose(1, 0, 2, 3)
    summed = seq_scatter(packed, 6)
    out_head = summed[:144].reshape(3, 48, 128).transpose(1, 0, 2).reshape(48, 384)
    return (
        track_loss,
        out_head,
        unpack_conv(summed[360:576], odd),
        unpack_conv(summed[144:360], odd),
    )


def solution(mesh):
    placed = (
        P("dp", "seq", None),
        P(None, "dp", None),
        P(None, "dp", None),
        P(None, "dp"),
        P(None, "seq", "dp"),
        P(),
    )
    return jax.shard_map(
        on_device,
        mesh=mesh,
        in_specs=placed,
        out_specs=(P(None, "dp"), P("seq", "dp"), P(None, "seq", "dp"), P(None, "seq", "dp")),
        check_vma=False,
    )
```

```python
import functools

import jax
import jax.numpy as jnp
from jax import lax
from jax.experimental import pallas as pl
from jax.experimental.pallas import tpu as pltpu
from jax.sharding import PartitionSpec as P

DMAX = 32
NZ = 8
MESH = pl.DeviceIdType.MESH
BF = jnp.bfloat16
F32 = jnp.float32


def remote(src, dst, send, recv, device):
    return pltpu.make_async_remote_copy(
        src_ref=src, dst_ref=dst, send_sem=send, recv_sem=recv, device_id=device, device_id_type=MESH
    )


def greet(devices):
    barrier = pltpu.get_barrier_semaphore()
    for device in devices:
        pl.semaphore_signal(barrier, inc=1, device_id=device, device_id_type=MESH)
    pl.semaphore_wait(barrier, len(devices))


def z_neighbours():
    z = lax.axis_index("dp")
    return z, lax.rem(z + 1, NZ), lax.rem(z + NZ - 1, NZ)


def seq_neighbours():
    s, n = lax.axis_index("seq"), lax.axis_size("seq")
    return s, lax.rem(s + 1, n), lax.rem(s + n - 1, n)


def ring_gather(own, slot, half_rows, send_sem, recv_sem, on_block):
    z, right, left = z_neighbours()
    copies = {}
    for way in (0, 1):
        sign = -1 if way == 0 else 1
        peer = {"dp": right if way == 0 else left}
        for step in range(4):
            block = lax.rem(z + sign * step + NZ, NZ)
            for half in (0, 1):
                if step == 3 and half != way:
                    continue
                source = own(half) if step == 0 else slot(block, half)
                copies[way, step, half] = remote(
                    source, slot(block, half), send_sem.at[way, step, half], recv_sem.at[way, step, half], peer
                )
    for half in (0, 1):
        for way in (0, 1):
            copies[way, 0, half].start()
    on_block(0, z)
    for step in (1, 2, 3):
        for half in (0, 1):
            for way in (0, 1):
                copies[way, step - 1, half].wait_recv()
                if (way, step, half) in copies:
                    copies[way, step, half].start()
        on_block(2 * step - 1, lax.rem(z - step + NZ, NZ))
        on_block(2 * step, lax.rem(z + step, NZ))
    copies[0, 3, 0].wait_recv()
    copies[1, 3, 1].wait_recv()
    on_block(7, lax.rem(z + 4, NZ))
    for copy in copies.values():
        copy.wait_send()


def rows_gather_kernel(x_ref, out_ref, send_sem, recv_sem, edge_send, edge_recv, own_sem):
    length = x_ref.shape[0]
    z, right, left = z_neighbours()
    s, after, before = seq_neighbours()
    greet([{"dp": right}, {"dp": left}, {"seq": after}, {"seq": before}])
    mine = pltpu.make_async_copy(x_ref, out_ref.at[z, pl.ds(DMAX, length)], own_sem)
    mine.start()
    half_rows = length // 2
    edges = []

    def on_block(order, block):
        if order == 0:
            first, last = x_ref.at[pl.ds(0, DMAX)], x_ref.at[pl.ds(length - DMAX, DMAX)]
        else:
            first, last = out_ref.at[block, pl.ds(DMAX, DMAX)], out_ref.at[block, pl.ds(length, DMAX)]
        for side, (src, dst, peer) in enumerate(
            (
                (last, out_ref.at[block, pl.ds(0, DMAX)], after),
                (first, out_ref.at[block, pl.ds(DMAX + length, DMAX)], before),
            )
        ):
            copy = remote(src, dst, edge_send.at[side, order], edge_recv.at[side, order], {"seq": peer})
            copy.start()
            edges.append(copy)

    ring_gather(
        lambda h: x_ref.at[pl.ds(h * half_rows, half_rows)],
        lambda k, h: out_ref.at[k, pl.ds(DMAX + h * half_rows, half_rows)],
        half_rows,
        send_sem,
        recv_sem,
        on_block,
    )
    for copy in edges:
        copy.wait_recv()
        copy.wait_send()
    mine.wait()

    @pl.when(s == 0)
    def _():
        out_ref[:, 0:DMAX, :] = jnp.zeros_like(out_ref[:, 0:DMAX, :])

    @pl.when(s == lax.axis_size("seq") - 1)
    def _():
        out_ref[:, length + DMAX :, :] = jnp.zeros_like(out_ref[:, length + DMAX :, :])


def whole(n):
    return [pl.BlockSpec(memory_space=pltpu.VMEM)] * n


def rows_gather(x, collective_id):
    length, width = x.shape
    return pl.pallas_call(
        rows_gather_kernel,
        out_shape=jax.ShapeDtypeStruct((NZ, length + 2 * DMAX, width), x.dtype),
        in_specs=whole(1),
        out_specs=whole(1)[0],
        scratch_shapes=[
            pltpu.SemaphoreType.DMA((2, 4, 2)),
            pltpu.SemaphoreType.DMA((2, 4, 2)),
            pltpu.SemaphoreType.DMA((2, 8)),
            pltpu.SemaphoreType.DMA((2, 8)),
            pltpu.SemaphoreType.DMA,
        ],
        compiler_params=pltpu.CompilerParams(collective_id=collective_id, has_side_effects=True),
        name="rows_gather",
    )(x)


LO, HI = slice(0, 64), slice(64, 128)
ROWS, PART, RIM = 1024, 512, 8 * DMAX
HALF = (ROWS + PART) // 2
CUBE = 0.044715
SLOPE = 0.7978845608028654


def activate_slope(value):
    square = value * value
    turn = jnp.tanh(SLOPE * (value + CUBE * value * square))
    return 0.5 * (1.0 + turn) + 0.5 * value * (1.0 - turn * turn) * (SLOPE * (1.0 + 3.0 * CUBE * square))


def greet_later(devices):
    barrier = pltpu.get_barrier_semaphore()
    for device in devices:
        pl.semaphore_signal(barrier, inc=1, device_id=device, device_id_type=MESH)
    return lambda: pl.semaphore_wait(barrier, len(devices))


def chunk(i, size):
    return pl.ds(pl.multiple_of(i * size, size), size)


def conv_chunk(framed, weight, spacing, index):
    total = None
    for tap in range(3):
        rows = framed[pl.ds(DMAX + (tap - 1) * spacing + 32 * index, 32)].reshape(256, 192 * NZ)
        term = lax.dot_general(rows, weight[tap], (((1,), (1,)), ((), ())), preferred_element_type=F32)
        total = term if total is None else total + term
    return total


def layer(framed, weight, spacing, base, pre_ref, hid_ref, held, z):
    @pl.loop(0, 2)
    def _(i):
        rests = []
        for index in (i, i + 2):
            pre = conv_chunk(framed, weight, spacing, index)
            hidden = (base(index).astype(F32) + jax.nn.gelu(pre)).astype(BF)
            pre_ref[chunk(index, 256), :] = pre
            if hid_ref is not None:
                hid_ref[chunk(index, 256), :] = hidden
            held[z, chunk(index, 256), :] = hidden[:, 0:128]
            rests.append(hidden[:, 128:192])
        held[z, pl.ds(pl.multiple_of(ROWS + 256 * i, 256), 256), :] = jnp.concatenate(rests, axis=1)


def ring_held(held, send_sem, recv_sem, on_block):
    z = lax.axis_index("dp")
    ring_gather(
        lambda h: held.at[z, pl.ds(h * HALF, HALF)],
        lambda k, h: held.at[k, pl.ds(h * HALF, HALF)],
        HALF,
        send_sem,
        recv_sem,
        on_block,
    )


def unpack(held, out_ref, base):
    for j in range(NZ // 2):
        one, two, lane = 2 * j, 2 * j + 1, 384 * j
        out_ref[base : base + ROWS, lane : lane + 128] = held[one, 0:ROWS, :]
        out_ref[base : base + ROWS, lane + 256 : lane + 384] = held[two, 0:ROWS, :]
        for h, lanes in ((0, LO), (1, HI)):
            out_ref[base + h * PART : base + (h + 1) * PART, lane + 128 : lane + 256] = jnp.concatenate(
                [held[one, ROWS : ROWS + PART, lanes], held[two, ROWS : ROWS + PART, lanes]], axis=1
            )


def first_kernel(
    gaps, fe_ref, w_ref, pre_ref, hid_ref, out_ref, held, edge, send_sem, recv_sem, edge_send, edge_recv
):
    z, right, left = z_neighbours()
    s, after, before = seq_neighbours()
    met = greet_later([{"dp": right}, {"dp": left}, {"seq": after}, {"seq": before}])
    odd = lax.rem(z, 2) == 1

    def base(index):
        rows = pl.ds(DMAX + 32 * index, 32)
        main = fe_ref[rows, :, pl.ds(pl.multiple_of(128 * (3 * (z // 2) + 2 * lax.rem(z, 2)), 128), 128)].reshape(256, 128)
        rest = fe_ref[rows, :, pl.ds(pl.multiple_of(128 * (3 * (z // 2) + 1), 128), 128)].reshape(256, 128)
        rest = jnp.where(odd, rest[:, HI].astype(F32), rest[:, LO].astype(F32))
        return jnp.concatenate([main.astype(F32), rest], axis=1)

    layer(fe_ref, w_ref, gaps[0], base, pre_ref, hid_ref, held, z)
    met()
    edges = []

    def on_block(order, block):
        for side, piece, at, peer in (
            (0, 0, ROWS - RIM, after),
            (0, 1, ROWS + PART - RIM, after),
            (1, 0, 0, before),
            (1, 1, ROWS, before),
        ):
            copy = remote(
                held.at[block, pl.ds(at, RIM)],
                edge.at[side, block, pl.ds(piece * RIM, RIM)],
                edge_send.at[side, piece, order],
                edge_recv.at[side, piece, order],
                {"seq": peer},
            )
            copy.start()
            edges.append(copy)

    ring_held(held, send_sem, recv_sem, on_block)
    unpack(held, out_ref, RIM)
    for copy in edges:
        copy.wait_recv()
        copy.wait_send()
    n = lax.axis_size("seq")
    for side, at, lanes, keep in ((0, 0, HI, s > 0), (1, RIM + ROWS, LO, s < n - 1)):
        for j in range(NZ // 2):
            one, two, lane = 2 * j, 2 * j + 1, 384 * j
            pieces = (
                edge[side, one, 0:RIM, :],
                jnp.concatenate([edge[side, one, RIM : 2 * RIM, lanes], edge[side, two, RIM : 2 * RIM, lanes]], axis=1),
                edge[side, two, 0:RIM, :],
            )
            for i, piece in enumerate(pieces):
                out_ref[at : at + RIM, lane + 128 * i : lane + 128 * (i + 1)] = jnp.where(
                    keep, piece, jnp.zeros_like(piece)
                )


SMEM = pl.BlockSpec(memory_space=pltpu.SMEM)


def call(kernel, name, collective_id, out_shapes, in_specs, scratch, *operands):
    return pl.pallas_call(
        kernel,
        out_shape=tuple(jax.ShapeDtypeStruct(*o) for o in out_shapes),
        in_specs=in_specs,
        out_specs=tuple(whole(len(out_shapes))),
        scratch_shapes=scratch,
        compiler_params=pltpu.CompilerParams(collective_id=collective_id, has_side_effects=True),
        name=name,
    )(*operands)


DMA = pltpu.SemaphoreType.DMA
PACKED = (ROWS + PART, 128)


def first_layer(gaps, framed_in, weight):
    return call(
        first_kernel,
        "first_layer",
        1,
        [((ROWS, 192), F32), ((ROWS, 192), BF), ((ROWS + 2 * RIM, 192 * NZ), BF)],
        [SMEM] + whole(2),
        [
            pltpu.VMEM((NZ, *PACKED), BF),
            pltpu.VMEM((2, NZ, 2 * RIM, 128), BF),
            DMA((2, 4, 2)),
            DMA((2, 4, 2)),
            DMA((2, 2, 8)),
            DMA((2, 2, 8)),
        ],
        gaps,
        framed_in,
        weight,
    )


def seq_place():
    s = lax.axis_index("seq")
    return s // 8, lax.rem(s // 2, 4), lax.rem(s, 2)


def seq_peers():
    y, x, core = seq_place()
    at = lambda y, x, core: (y * 4 + x) * 2 + core
    other = at(y, x, 1 - core)
    along_x = [at(y, lax.rem(x + d, 4), core) for d in (1, 2, 3)]
    along_y = [at(lax.rem(y + d, 4), x, core) for d in (1, 2, 3)]
    return other, along_x, along_y


def merge_stats(stats, merged, got, send_sem, recv_sem, own_sem):
    y, x, core = seq_place()
    other, along_x, along_y = seq_peers()
    stages = ((2, core, [other]), (4, x, along_x), (4, y, along_y))
    for number, (count, place, peers) in enumerate(stages):
        source = stats if number == 0 else merged.at[number - 1]
        copies = []
        for d, peer in enumerate(peers):
            copy = remote(
                source, got.at[number, place], send_sem.at[number, d], recv_sem.at[number, d], {"seq": peer}
            )
            copy.start()
            copies.append(copy)
        mine = pltpu.make_async_copy(source, got.at[number, place], own_sem.at[number])
        mine.start()
        mine.wait()
        for copy in copies:
            copy.wait_recv()
        peak = got[number, 0, 0]
        for i in range(1, count):
            peak = jnp.maximum(peak, got[number, i, 0])
        sums = [jnp.zeros_like(peak) for _ in range(3)]
        for i in range(count):
            sums[0] = sums[0] + got[number, i, 1] * jnp.exp(got[number, i, 0] - peak)
            sums[1] = sums[1] + got[number, i, 2]
            sums[2] = sums[2] + got[number, i, 3]
        for copy in copies:
            copy.wait_send()
        if number < 2:
            merged[number, 0] = peak
            for i in range(3):
                merged[number, i + 1] = sums[i]
    return peak, *sums


def second_kernel(
    gaps,
    f_ref,
    w_ref,
    hid_ref,
    head_ref,
    counts_ref,
    pre_ref,
    out_ref,
    grad_ref,
    loss_ref,
    held,
    logits,
    targets,
    stats,
    merged,
    got,
    send_sem,
    recv_sem,
    stat_send,
    stat_recv,
    stat_own,
):
    z, right, left = z_neighbours()
    other, along_x, along_y = seq_peers()
    met = greet_later([{"dp": right}, {"dp": left}] + [{"seq": p} for p in [other, *along_x, *along_y]])
    layer(f_ref, w_ref, gaps[1], lambda index: hid_ref[chunk(index, 256), :], pre_ref, None, held, z)
    met()

    def on_block(order, block):
        if order in (1, 3):

            @pl.loop(4 * (order - 1), 4 * (order + 1))
            def _(i):
                targets[chunk(i, 8)] = jnp.swapaxes(counts_ref[:, chunk(i, 8), :], 0, 1).astype(F32)

    ring_held(held, send_sem, recv_sem, on_block)
    unpack(held, out_ref, 0)
    shape = stats.shape[1:]

    def forward(i, carry):
        peak, count, cross = carry
        value = jnp.dot(out_ref[chunk(i, 256), :], head_ref[...], preferred_element_type=F32).reshape(32, *shape)
        logits[chunk(i, 32)] = value
        target = targets[chunk(i, 32)]
        return (
            jnp.maximum(peak, jnp.max(value, axis=0)),
            count + jnp.sum(target, axis=0),
            cross + jnp.sum(target * value, axis=0),
        )

    zero = jnp.zeros(shape, F32)
    peak, count, cross = lax.fori_loop(0, 4, forward, (jnp.full(shape, -jnp.inf, F32), zero, zero))
    spread = lax.fori_loop(
        0, 8, lambda i, t: t + jnp.sum(jnp.exp(logits[chunk(i, 16)] - peak[None]), axis=0), zero
    )
    for i, value in enumerate((peak, spread, count, cross)):
        stats[i] = value
    peak, spread, count, cross = merge_stats(stats, merged, got, stat_send, stat_recv, stat_own)
    lse = peak + jnp.log(spread)
    bins = 128 * lax.axis_size("seq")
    loss_ref[...] = (count * lse - cross) / bins

    @pl.loop(0, 8)
    def _(i):
        value = (count[None] * jnp.exp(logits[chunk(i, 16)] - lse[None]) - targets[chunk(i, 16)]) * (1.0 / bins)
        grad_ref[chunk(i, 128), :] = value.reshape(128, shape[1]).astype(BF)


def second_layer(gaps, framed_one, weight, hidden_one, head_weight, counts):
    tracks = head_weight.shape[1]
    stat = (4, NZ, tracks)
    return call(
        second_kernel,
        "second_layer",
        2,
        [((ROWS, 192), F32), ((ROWS, 192 * NZ), BF), ((ROWS, tracks), BF), ((NZ, tracks), F32)],
        [SMEM] + whole(5),
        [
            pltpu.VMEM((NZ, *PACKED), BF),
            pltpu.VMEM((128, NZ, tracks), F32),
            pltpu.VMEM((128, NZ, tracks), F32),
            pltpu.VMEM(stat, F32),
            pltpu.VMEM((2, *stat), F32),
            pltpu.VMEM((3, 4, *stat), F32),
            DMA((2, 4, 2)),
            DMA((2, 4, 2)),
            DMA((3, 3)),
            DMA((3, 3)),
            DMA((3,)),
        ],
        gaps,
        framed_one,
        weight,
        hidden_one,
        head_weight,
        counts,
    )


def ring_scatter(own, got, sent, send_sem, recv_sem, pair_of, hook):
    z, right, left = z_neighbours()
    piece = lambda h: pl.ds(h * HALF, HALF)
    far = lax.rem(z + 4, NZ) // 2
    pair_of(far)
    copies = {}
    for step in range(4):
        for half in (0, 1):
            for way in (0, 1):
                if step == 0 and half != way:
                    continue
                sign = 1 if way == 0 else -1
                block = lax.rem(z + sign * (4 - step) + NZ, NZ)
                before = copies.get((way, step - 1, half))
                if before is None:
                    source = own.at[block, piece(half)]
                else:
                    before.wait_recv()
                    sent[way, step - 1, piece(half), :] = (
                        got[way, step - 1, piece(half), :].astype(F32) + own[block, piece(half), :].astype(F32)
                    ).astype(BF)
                    source = sent.at[way, step - 1, piece(half)]
                copy = remote(
                    source,
                    got.at[way, step, piece(half)],
                    send_sem.at[way, step, half],
                    recv_sem.at[way, step, half],
                    {"dp": right if way == 0 else left},
                )
                copy.start()
                copies[way, step, half] = copy
        if step == 0:
            for d in (1, 3, 2):
                pair_of(lax.rem(far + d, NZ // 2))
        hook(step)
    for half in (0, 1):
        copies[0, 3, half].wait_recv()
        copies[1, 3, half].wait_recv()
    for copy in copies.values():
        copy.wait_send()


def ring_total(own, got, at, size):
    z = lax.axis_index("dp")
    rows = pl.ds(pl.multiple_of(at, 256), size)
    return own[z, rows, :].astype(F32) + got[0, 3, rows, :].astype(F32) + got[1, 3, rows, :].astype(F32)


def ring_result(own, got, i):
    rest = ring_total(own, got, ROWS + 256 * i, 256)
    return [
        (index, jnp.concatenate([ring_total(own, got, 256 * index, 256), rest[:, lanes]], axis=1))
        for index, lanes in ((i, LO), (i + 2, HI))
    ]


def put_pair(own, pair, i, product):
    one, two = 2 * pair, 2 * pair + 1
    for index, value in zip((i, i + 2), product):
        own[one, chunk(index, 256), :] = value[:, 0:128]
        own[two, chunk(index, 256), :] = value[:, 256:384]
    rows = pl.ds(pl.multiple_of(ROWS + 256 * i, 256), 256)
    low, high = product
    own[one, rows, :] = jnp.concatenate([low[:, 128:192], high[:, 128:192]], axis=1)
    own[two, rows, :] = jnp.concatenate([low[:, 192:256], high[:, 192:256]], axis=1)


class Spread:
    def __init__(self, source, result, first, number, scratch):
        self.source, self.result, self.first, self.number = source, result, first, number
        self.pair, self.both, self.got_one, self.mid, self.got_two, self.send, self.recv = scratch
        self.y, self.x, self.core = seq_place()
        self.other, self.along_x, self.along_y = seq_peers()

    def stage(self, which):
        along = self.first if which == 1 else ("y" if self.first == "x" else "x")
        return (self.x, self.along_x) if along == "x" else (self.y, self.along_y)

    def copy(self, source, target, slot, peer):
        made = remote(source, target, self.send.at[self.number, slot], self.recv.at[self.number, slot], {"seq": peer})
        made.start()
        return made

    def begin(self):
        self.exchange = self.copy(self.source(1 - self.core), self.pair, 0, self.other)

    def add_pair(self):
        self.exchange.wait_recv()
        mine = self.source(self.core)

        @pl.loop(0, 16)
        def _(i):
            spot = lax.rem(i, 4) * 4 + i // 4 if self.first == "x" else i
            self.both[spot] = (self.pair[i].astype(F32) + mine[i].astype(F32)).astype(BF)

        place, peers = self.stage(1)
        self.copies = []
        for d, peer in enumerate(peers):
            target = lax.rem(place + d + 1, 4)
            self.copies.append(self.copy(self.both.at[pl.ds(4 * target, 4)], self.got_one.at[2 - d], 1 + d, peer))

    def add_first(self):
        for copy in self.copies:
            copy.wait_recv()
        place, _ = self.stage(1)

        @pl.loop(0, 4)
        def _(i):
            total = self.both[4 * place + i].astype(F32)
            for d in range(3):
                total = total + self.got_one[d, i].astype(F32)
            self.mid[i] = total.astype(BF)

        place, peers = self.stage(2)
        self.later = []
        for d, peer in enumerate(peers):
            target = lax.rem(place + d + 1, 4)
            self.later.append(self.copy(self.mid.at[target], self.got_two.at[2 - d], 4 + d, peer))

    def finish(self):
        for copy in self.later:
            copy.wait_recv()
        place, _ = self.stage(2)
        total = self.mid[place].astype(F32)
        for d in range(3):
            total = total + self.got_two[d].astype(F32)
        self.result[...] = total
        for copy in [self.exchange, *self.copies, *self.later]:
            copy.wait_send()


def spread_scratch(rows, width):
    return [
        pltpu.VMEM((16, rows, width), BF),
        pltpu.VMEM((16, rows, width), BF),
        pltpu.VMEM((3, 4, rows, width), BF),
        pltpu.VMEM((4, rows, width), BF),
        pltpu.VMEM((3, rows, width), BF),
    ]


def ring_scratch():
    return [
        pltpu.VMEM((NZ, *PACKED), BF),
        pltpu.VMEM((2, 4, *PACKED), BF),
        pltpu.VMEM((2, 3, *PACKED), BF),
        DMA((2, 4, 2)),
        DMA((2, 4, 2)),
    ]


def seq_hellos():
    other, along_x, along_y = seq_peers()
    return [other, *along_x, *along_y]


def third_kernel(
    grad_ref,
    head_ref,
    rows_ref,
    pre_ref,
    back_ref,
    up_ref,
    head_out,
    own,
    got,
    sent,
    send_sem,
    recv_sem,
    head_grad,
    pair,
    both,
    got_one,
    mid,
    got_two,
    spread_send,
    spread_recv,
    edge_send,
    edge_recv,
):
    z, right, left = z_neighbours()
    s, after, before = seq_neighbours()
    met = greet_later(
        [{"dp": right}, {"dp": left}, {"seq": after}, {"seq": before}] + [{"seq": p} for p in seq_hellos()]
    )
    started = []

    def pair_of(p):
        @pl.loop(0, 2)
        def _(i):
            product = [
                lax.dot_general(
                    grad_ref[chunk(index, 256), :],
                    head_ref[chunk(p, 384), :],
                    (((1,), (1,)), ((), ())),
                    preferred_element_type=F32,
                ).astype(BF)
                for index in (i, i + 2)
            ]
            put_pair(own, p, i, product)

        if not started:
            met()
            started.append(1)

    scratch = (pair, both, got_one, mid, got_two, spread_send, spread_recv)
    spread = Spread(lambda core: head_grad.at[:, core], head_out, "x", 0, scratch)

    def hook(step):
        if step == 0:

            @pl.loop(0, 4)
            def _(c):
                value = lax.dot_general(
                    rows_ref[:, chunk(c, 384)], grad_ref[...], (((0,), (0,)), ((), ())), preferred_element_type=F32
                )
                head_grad[chunk(c, 4)] = value.astype(BF).reshape(4, 2, 48, value.shape[1])

            spread.begin()
        elif step == 1:
            spread.add_pair()
        elif step == 2:
            spread.add_first()
        else:
            spread.finish()

    ring_scatter(own, got, sent, send_sem, recv_sem, pair_of, hook)

    @pl.loop(0, 2)
    def _(i):
        for index, value in ring_result(own, got, i):
            back_ref[chunk(index, 256), :] = value
            up = (value * activate_slope(pre_ref[chunk(index, 256), :])).astype(BF)
            up_ref[pl.ds(DMAX + 32 * index, 32)] = up.reshape(32, NZ, 192)

    edges = []
    for side, (src, dst, peer) in enumerate(((128, 0, after), (DMAX, DMAX + 128, before))):
        copy = remote(
            up_ref.at[pl.ds(src, DMAX)], up_ref.at[pl.ds(dst, DMAX)], edge_send.at[side], edge_recv.at[side], {"seq": peer}
        )
        copy.start()
        edges.append(copy)
    for copy in edges:
        copy.wait_recv()
        copy.wait_send()
    for at, drop in ((0, s == 0), (DMAX + 128, s == lax.axis_size("seq") - 1)):

        @pl.when(drop)
        def _():
            up_ref[at : at + DMAX] = jnp.zeros_like(up_ref[at : at + DMAX])


def third_layer(logit_grad, head_weight, head_rows, pre_two):
    tracks = head_weight.shape[1]
    return call(
        third_kernel,
        "third_layer",
        3,
        [((ROWS, 192), F32), ((128 + 2 * DMAX, NZ, 192), BF), ((48, tracks), F32)],
        whole(4),
        ring_scratch()
        + [pltpu.VMEM((16, 2, 48, tracks), BF)]
        + spread_scratch(48, tracks)
        + [DMA((1, 7)), DMA((1, 7)), DMA((2,)), DMA((2,))],
        logit_grad,
        head_weight,
        head_rows,
        pre_two,
    )


def tap_grad(framed, spacing, up, tap, into):
    @pl.loop(0, 4)
    def _(c):
        rows = framed[pl.ds(DMAX + (tap - 1) * spacing, 128), :, chunk(c, 384)].reshape(ROWS, 384)
        value = lax.dot_general(rows, up, (((0,), (0,)), ((), ())), preferred_element_type=F32)
        into[chunk(c, 4)] = value.astype(BF).reshape(4, 2, 48, 192)


def fourth_kernel(
    gaps,
    up_ref,
    w_ref,
    back_ref,
    pre_ref,
    f_ref,
    one_ref,
    two_out,
    own,
    got,
    sent,
    send_sem,
    recv_sem,
    grads,
    pair,
    both,
    got_one,
    mid,
    got_two,
    spread_send,
    spread_recv,
):
    z, right, left = z_neighbours()
    met = greet_later([{"dp": right}, {"dp": left}] + [{"seq": p} for p in seq_hellos()])
    gap = gaps[1]
    started = []

    def pair_of(p):
        @pl.loop(0, 2)
        def _(i):
            product = []
            for index in (i, i + 2):
                total = None
                for tap in range(3):
                    rows = up_ref[pl.ds(DMAX - (tap - 1) * gap + 32 * index, 32)].reshape(256, 192)
                    term = jnp.dot(rows, w_ref[tap, :, chunk(p, 384)], preferred_element_type=F32)
                    total = term if total is None else total + term
                product.append(total.astype(BF))
            put_pair(own, p, i, product)

        if not started:
            met()
            started.append(1)

    spreads = [
        Spread(
            lambda core, t=t: grads.at[t, :, core],
            two_out.at[t],
            "xyx"[t],
            t,
            tuple(r.at[t] for r in (pair, both, got_one, mid, got_two)) + (spread_send, spread_recv),
        )
        for t in range(3)
    ]

    def hook(step):
        up = lambda: up_ref[DMAX : DMAX + 128].reshape(ROWS, 192)
        if step == 0:
            tap_grad(f_ref, gap, up(), 0, grads.at[0])
            spreads[0].begin()
        elif step == 1:
            tap_grad(f_ref, gap, up(), 1, grads.at[1])
            spreads[1].begin()
            tap_grad(f_ref, gap, up(), 2, grads.at[2])
            spreads[2].begin()
        elif step == 2:
            for t in range(3):
                spreads[t].add_pair()
        else:
            for t in range(3):
                spreads[t].add_first()

    ring_scatter(own, got, sent, send_sem, recv_sem, pair_of, hook)

    @pl.loop(0, 2)
    def _(i):
        for index, value in ring_result(own, got, i):
            rows = chunk(index, 256)
            one_ref[rows, :] = ((back_ref[rows, :] + value) * activate_slope(pre_ref[rows, :])).astype(BF)

    for t in range(3):
        spreads[t].finish()


def fourth_layer(gaps, framed_up, weight, back, pre_one, framed_one):
    taps = lambda shapes: [pltpu.VMEM((3, *s.shape), s.dtype) for s in shapes]
    return call(
        fourth_kernel,
        "fourth_layer",
        4,
        [((ROWS, 192), BF), ((3, 48, 192), F32)],
        [SMEM] + whole(5),
        ring_scratch()
        + [pltpu.VMEM((3, 16, 2, 48, 192), BF)]
        + taps(spread_scratch(48, 192))
        + [DMA((3, 7)), DMA((3, 7))],
        gaps,
        framed_up,
        weight,
        back,
        pre_one,
        framed_one,
    )


def fifth_kernel(
    gaps, fe_ref, up_ref, one_out, grads, pair, both, got_one, mid, got_two, spread_send, spread_recv
):
    met = greet_later([{"seq": p} for p in seq_hellos()])
    spreads = [
        Spread(
            lambda core, t=t: grads.at[t, :, core],
            one_out.at[t],
            "xyx"[t],
            t,
            tuple(r.at[t] for r in (pair, both, got_one, mid, got_two)) + (spread_send, spread_recv),
        )
        for t in range(3)
    ]
    for t in range(3):
        tap_grad(fe_ref, gaps[0], up_ref[...], t, grads.at[t])
        if t == 0:
            met()
        spreads[t].begin()
    for t in range(3):
        spreads[t].add_pair()
    for t in range(3):
        spreads[t].add_first()
    for t in range(3):
        spreads[t].finish()


def fifth_layer(gaps, framed_in, up_one):
    taps = lambda shapes: [pltpu.VMEM((3, *s.shape), s.dtype) for s in shapes]
    return call(
        fifth_kernel,
        "fifth_layer",
        5,
        [((3, 48, 192), F32)],
        [SMEM] + whole(2),
        [pltpu.VMEM((3, 16, 2, 48, 192), BF)] + taps(spread_scratch(48, 192)) + [DMA((3, 7)), DMA((3, 7))],
        gaps,
        framed_in,
        up_one,
    )[0]


def on_device(embeddings, conv_one, conv_two, head_weight, counts, dilation):
    odd = lax.rem(lax.axis_index("dp"), 2) == 1
    turn = lambda w: jnp.where(odd, jnp.concatenate([w[:, 64:], w[:, :64]], axis=1), w)
    back_turn = lambda g: jnp.where(odd, jnp.concatenate([g[..., 128:], g[..., :128]], axis=-1), g)
    w_one, w_two = turn(conv_one), turn(conv_two)
    framed_in = jnp.transpose(rows_gather(embeddings[0], 0), (1, 0, 2))
    pre_one, hidden_one, framed_one = first_layer(dilation, framed_in, w_one)
    framed_one = framed_one.reshape(framed_in.shape)
    pre_two, head_rows, logit_grad, track_loss = second_layer(
        dilation, framed_one, w_two, hidden_one, head_weight, counts
    )
    grad_two_out, framed_up, grad_head = third_layer(logit_grad, head_weight, head_rows, pre_two)
    up_one, grad_two = fourth_layer(dilation, framed_up, w_two, grad_two_out, pre_one, framed_one)
    grad_one = fifth_layer(dilation, framed_in, up_one)
    return (track_loss, grad_head, back_turn(grad_one), back_turn(grad_two))


def solution(mesh):
    placed = (
        P("dp", "seq", None),
        P(None, "dp", None),
        P(None, "dp", None),
        P(None, "dp"),
        P(None, "seq", "dp"),
        P(),
    )
    return jax.shard_map(
        on_device,
        mesh=mesh,
        in_specs=placed,
        out_specs=(P(None, "dp"), P("seq", "dp"), P(None, "seq", "dp"), P(None, "seq", "dp")),
        check_vma=False,
    )
```

```python
import functools

import jax
import jax.numpy as jnp
from jax import lax
from jax.experimental import pallas as pl
from jax.experimental.pallas import tpu as pltpu
from jax.sharding import PartitionSpec as P

DMAX = 32
NZ = 8
MESH = pl.DeviceIdType.MESH
BF = jnp.bfloat16
F32 = jnp.float32


def remote(src, dst, send, recv, device):
    return pltpu.make_async_remote_copy(
        src_ref=src, dst_ref=dst, send_sem=send, recv_sem=recv, device_id=device, device_id_type=MESH
    )


def greet(devices):
    barrier = pltpu.get_barrier_semaphore()
    for device in devices:
        pl.semaphore_signal(barrier, inc=1, device_id=device, device_id_type=MESH)
    pl.semaphore_wait(barrier, len(devices))


def z_neighbours():
    z = lax.axis_index("dp")
    return z, lax.rem(z + 1, NZ), lax.rem(z + NZ - 1, NZ)


def seq_neighbours():
    s, n = lax.axis_index("seq"), lax.axis_size("seq")
    return s, lax.rem(s + 1, n), lax.rem(s + n - 1, n)


def whole(n):
    return [pl.BlockSpec(memory_space=pltpu.VMEM)] * n


LO, HI = slice(0, 64), slice(64, 128)
ROWS, PART, RIM = 1024, 512, 8 * DMAX
HALF = (ROWS + PART) // 2
CUBE = 0.044715
SLOPE = 0.7978845608028654


def activate_slope(value):
    square = value * value
    turn = jnp.tanh(SLOPE * (value + CUBE * value * square))
    return 0.5 * (1.0 + turn) + 0.5 * value * (1.0 - turn * turn) * (SLOPE * (1.0 + 3.0 * CUBE * square))


def greet_later(devices):
    barrier = pltpu.get_barrier_semaphore()
    for device in devices:
        pl.semaphore_signal(barrier, inc=1, device_id=device, device_id_type=MESH)
    return lambda: pl.semaphore_wait(barrier, len(devices))


def chunk(i, size):
    return pl.ds(pl.multiple_of(i * size, size), size)


def natural(odd, main, rest):
    return jnp.where(odd, jnp.concatenate([rest, main], axis=1), jnp.concatenate([main, rest], axis=1))


def put_chunk(held, z, slot, hidden):
    odd = lax.rem(z, 2) == 1
    main = jnp.where(odd, hidden[:, 64:192], hidden[:, 0:128])
    rest = jnp.where(odd, hidden[:, 0:64], hidden[:, 128:192])
    held[z, slot, 0:256, :] = main.astype(BF)
    held[z, slot, 256:384, :] = jnp.concatenate([rest[0:128], rest[128:256]], axis=1).astype(BF)


def ring_gather(slot, send_sem, recv_sem, make, on_chunk, on_step, own=None):
    z, right, left = z_neighbours()
    copies = {}

    def start(way, step, c):
        block = lax.rem(z + (-step if way == 0 else step) + NZ, NZ)
        source = own(c) if step == 0 and own else slot(block, c)
        copy = remote(
            source, slot(block, c), send_sem.at[way, step, c], recv_sem.at[way, step, c], {"dp": right if way == 0 else left}
        )
        copy.start()
        copies[way, step, c] = copy

    for c in range(4):
        make(c)
        for way in (0, 1):
            start(way, 0, c)
        on_chunk(0, z, c)
    for step in (1, 2, 3):
        for c in range(4):
            for way in (0, 1):
                copies[way, step - 1, c].wait_recv()
                if step < 3 or c // 2 == way:
                    start(way, step, c)
            on_chunk(2 * step - 1, lax.rem(z - step + NZ, NZ), c)
            on_chunk(2 * step, lax.rem(z + step, NZ), c)
        on_step(step)
    for c in (0, 2, 1, 3):
        copies[c // 2, 3, c].wait_recv()
        on_chunk(7, lax.rem(z + 4, NZ), c)
    on_step(4)
    for copy in copies.values():
        copy.wait_send()


def pair_order(z):
    own, sign = z // 2, 2 * lax.rem(z, 2) - 1
    return [lax.rem(own + d + 4, 4) for d in (0, sign, -sign, 2)]


def unpack_slot(held, pair, slot, put):
    one, two = 2 * pair, 2 * pair + 1
    low, high = held[one, slot, 256:384, :], held[two, slot, 256:384, :]
    mid = jnp.concatenate(
        [jnp.concatenate([low[:, h], high[:, h]], axis=1) for h in (LO, HI)],
        axis=0,
    )
    for i, value in enumerate((held[one, slot, 0:256, :], mid, held[two, slot, 0:256, :])):
        put(pl.ds(pl.multiple_of(384 * pair + 128 * i, 128), 128), value)


def first_kernel(
    gaps,
    x_ref,
    w_ref,
    w_two_ref,
    fe_ref,
    pre_ref,
    hid_ref,
    out_ref,
    pre_two_ref,
    rows_held,
    pre_rows,
    hid_rows,
    held,
    send_sem,
    recv_sem,
    edge_send,
    edge_recv,
    own_sem,
):
    z, right, left = z_neighbours()
    s, after, before = seq_neighbours()
    n = lax.axis_size("seq")
    odd = lax.rem(z, 2) == 1
    mine = pltpu.make_async_copy(x_ref, rows_held.at[z, pl.ds(DMAX, 128)], own_sem)
    mine.start()
    greet_later([{"dp": right}, {"dp": left}, {"seq": after}, {"seq": before}])()
    rims = {}

    def rows_slot(k, c):
        return rows_held.at[k, pl.ds(DMAX + 32 * c, 32)]

    def own_rows(c):
        return x_ref.at[pl.ds(32 * c, 32)]

    def on_rows(order, block, c):
        for at, side, row, peer in ((3, 0, 0, after), (0, 1, DMAX + 128, before)):
            if c == at:
                copy = remote(
                    own_rows(c) if order == 0 else rows_slot(block, c),
                    rows_held.at[block, pl.ds(row, DMAX)],
                    edge_send.at[0, side, order],
                    edge_recv.at[0, side, order],
                    {"seq": peer},
                )
                copy.start()
                rims[side, order] = copy

    def convolve(order):
        shift = (0, -1, 1, -2, 2, -3, 3, 4)[order]
        block = lax.rem(z + shift + NZ, NZ)
        if order == 0:
            mine.wait()
        for side in (0, 1):
            rims[side, order].wait_recv()
        for drop, row in ((s == 0, 0), (s == n - 1, DMAX + 128)):

            @pl.when(drop)
            def _():
                rows_held[block, row : row + DMAX, :] = jnp.zeros((DMAX, 192 * NZ), BF)

        rows = rows_held[block]
        pre = None
        for tap in range(3):
            term = lax.dot_general(rows, w_ref[tap], (((1,), (1,)), ((), ())), preferred_element_type=F32)
            if tap == 1:
                term = term[DMAX : DMAX + 128]
            else:
                first = DMAX + (tap - 1) * gaps[0]
                term = pltpu.roll(term, lax.rem(192 - first, 192), 0)[0:128]
            pre = term if pre is None else pre + term
        main_at, rest_at = 3 * (z // 2) + 2 * lax.rem(z, 2), 3 * (z // 2) + 1
        main = rows_held[block, DMAX : DMAX + 128, pl.ds(pl.multiple_of(128 * main_at, 128), 128)].astype(F32)
        rest = rows_held[block, DMAX : DMAX + 128, pl.ds(pl.multiple_of(128 * rest_at, 128), 128)].astype(F32)
        own = natural(odd, main, jnp.where(odd, rest[:, HI], rest[:, LO]))
        pre_rows[block] = pre
        hid_rows[block] = own + jax.nn.gelu(pre)

    def on_rows_step(step):
        orders = {1: (0,), 2: (1, 2), 3: (3, 4, 5, 6), 4: (7,)}[step]
        for order in orders:
            convolve(order)

    ring_gather(
        rows_slot, send_sem.at[0], recv_sem.at[0], lambda c: None, on_rows, on_rows_step, own_rows
    )
    for copy in rims.values():
        copy.wait_send()

    def make(c):
        bins = slice(32 * c, 32 * c + 32)
        hidden = jnp.swapaxes(hid_rows[:, bins, :], 0, 1).reshape(256, 192)
        hid_ref[256 * c : 256 * c + 256, :] = hidden.astype(BF)
        put_chunk(held, z, 1 + c, hidden)

    edges = {}

    def on_chunk(order, block, c):
        for at, side, slot, peer in ((3, 0, 0, after), (0, 1, 5, before)):
            if c == at:
                copy = remote(
                    held.at[block, 1 + c],
                    held.at[block, slot],
                    edge_send.at[1, side, order],
                    edge_recv.at[1, side, order],
                    {"seq": peer},
                )
                copy.start()
                edges[side, order] = copy

    pairs = pair_order(z)

    def feed(number, orders):
        pair = pairs[number]
        for order in orders:
            for side in (0, 1):
                edges[side, order].wait_recv()

        @pl.loop(0, 6)
        def _(slot):
            keep = jnp.logical_and(jnp.logical_or(slot > 0, s > 0), jnp.logical_or(slot < 5, s < n - 1))

            def put(lanes, value):
                value = jnp.where(keep, value, jnp.zeros_like(value))
                out_ref[chunk(slot, 32), :, lanes] = value.reshape(32, NZ, 128)

            unpack_slot(held, pair, slot, put)

        lanes = chunk(pair, 384)

        @pl.loop(0, 4)
        def _(i):
            total = None
            for tap in range(3):
                rows = out_ref[pl.ds(DMAX + (tap - 1) * gaps[1] + 32 * i, 32), :, lanes].reshape(256, 384)
                term = lax.dot_general(rows, w_two_ref[tap, :, lanes], (((1,), (1,)), ((), ())), preferred_element_type=F32)
                total = term if total is None else total + term
            at = chunk(i, 256)
            pre_two_ref[at, :] = total if number == 0 else pre_two_ref[at, :] + total

    def to_bins(first, last):
        @pl.loop(first, last)
        def _(i):
            fe_ref[chunk(i, 16)] = jnp.swapaxes(rows_held[:, chunk(i, 16), :], 0, 1)

    def on_step(step):
        if step == 1:
            to_bins(0, 7)

            @pl.loop(0, 4)
            def _(i):
                pre_ref[chunk(i, 256), :] = jnp.swapaxes(pre_rows[:, chunk(i, 32), :], 0, 1).reshape(256, 192)

        elif step == 2:
            feed(0, (0, 1, 2))
            to_bins(7, 12)
        elif step == 3:
            feed(1, (3, 4))
            feed(2, (5, 6))
        elif step == 4:
            feed(3, (7,))

    ring_gather(lambda k, c: held.at[k, 1 + c], send_sem.at[1], recv_sem.at[1], make, on_chunk, on_step)
    for copy in edges.values():
        copy.wait_send()


SMEM = pl.BlockSpec(memory_space=pltpu.SMEM)


def call(kernel, name, collective_id, out_shapes, in_specs, scratch, *operands):
    return pl.pallas_call(
        kernel,
        out_shape=tuple(jax.ShapeDtypeStruct(*o) for o in out_shapes),
        in_specs=in_specs,
        out_specs=tuple(whole(len(out_shapes))),
        scratch_shapes=scratch,
        compiler_params=pltpu.CompilerParams(collective_id=collective_id, has_side_effects=True),
        name=name,
    )(*operands)


DMA = pltpu.SemaphoreType.DMA
PACKED = (ROWS + PART, 128)


def first_layer(gaps, rows, weight, weight_two):
    width = rows.shape[1]
    return call(
        first_kernel,
        "first_layer",
        1,
        [
            ((128 + 2 * DMAX, NZ, width), BF),
            ((ROWS, 192), F32),
            ((ROWS, 192), BF),
            ((128 + 2 * DMAX, NZ, width), BF),
            ((ROWS, 192), F32),
        ],
        [SMEM] + whole(3),
        [
            pltpu.VMEM((NZ, 128 + 2 * DMAX, width), BF),
            pltpu.VMEM((NZ, 128, 192), F32),
            pltpu.VMEM((NZ, 128, 192), F32),
            pltpu.VMEM((NZ, 6, 384, 128), BF),
            DMA((2, 2, 4, 4)),
            DMA((2, 2, 4, 4)),
            DMA((2, 2, 8)),
            DMA((2, 2, 8)),
            DMA,
        ],
        gaps,
        rows,
        weight,
        weight_two,
    )


def seq_place():
    s = lax.axis_index("seq")
    return s // 8, lax.rem(s // 2, 4), lax.rem(s, 2)


def seq_peers():
    y, x, core = seq_place()
    at = lambda y, x, core: (y * 4 + x) * 2 + core
    other = at(y, x, 1 - core)
    along_x = [at(y, lax.rem(x + d, 4), core) for d in (1, 2, 3)]
    along_y = [at(lax.rem(y + d, 4), x, core) for d in (1, 2, 3)]
    return other, along_x, along_y


def merge_stats(stats, merged, got, send_sem, recv_sem, own_sem):
    y, x, core = seq_place()
    other, along_x, along_y = seq_peers()
    stages = ((2, core, [other]), (4, x, along_x), (4, y, along_y))
    for number, (count, place, peers) in enumerate(stages):
        source = stats if number == 0 else merged.at[number - 1]
        copies = []
        for d, peer in enumerate(peers):
            copy = remote(
                source, got.at[number, place], send_sem.at[number, d], recv_sem.at[number, d], {"seq": peer}
            )
            copy.start()
            copies.append(copy)
        mine = pltpu.make_async_copy(source, got.at[number, place], own_sem.at[number])
        mine.start()
        mine.wait()
        for copy in copies:
            copy.wait_recv()
        peak = got[number, 0, 0]
        for i in range(1, count):
            peak = jnp.maximum(peak, got[number, i, 0])
        sums = [jnp.zeros_like(peak) for _ in range(3)]
        for i in range(count):
            sums[0] = sums[0] + got[number, i, 1] * jnp.exp(got[number, i, 0] - peak)
            sums[1] = sums[1] + got[number, i, 2]
            sums[2] = sums[2] + got[number, i, 3]
        for copy in copies:
            copy.wait_send()
        if number < 2:
            merged[number, 0] = peak
            for i in range(3):
                merged[number, i + 1] = sums[i]
    return peak, *sums


def second_kernel(
    pre_ref,
    hid_ref,
    head_ref,
    counts_ref,
    out_ref,
    grad_ref,
    loss_ref,
    held,
    logits,
    targets,
    stats,
    merged,
    got,
    send_sem,
    recv_sem,
    stat_send,
    stat_recv,
    stat_own,
):
    z, right, left = z_neighbours()
    other, along_x, along_y = seq_peers()
    met = greet_later([{"dp": right}, {"dp": left}] + [{"seq": p} for p in [other, *along_x, *along_y]])
    shape = stats.shape[1:]

    def make(c):
        rows = slice(256 * c, 256 * c + 256)
        put_chunk(held, z, c, hid_ref[rows, :].astype(F32) + jax.nn.gelu(pre_ref[rows, :]))
        if c == 0:
            met()

    pairs = pair_order(z)

    def feed(number):
        pair = pairs[number]
        lanes = chunk(pair, 384)

        @pl.loop(0, 4)
        def _(i):
            rows = chunk(i, 256)

            def put(at, value):
                out_ref[rows, at] = value

            unpack_slot(held, pair, i, put)
            value = jnp.dot(out_ref[rows, lanes], head_ref[lanes, :], preferred_element_type=F32).reshape(32, *shape)
            logits[chunk(i, 32)] = value if number == 0 else logits[chunk(i, 32)] + value

    def on_step(step):
        feed(step - 1)
        if step in (1, 2):

            @pl.loop(8 * (step - 1), 8 * step)
            def _(i):
                targets[chunk(i, 8)] = jnp.swapaxes(counts_ref[:, chunk(i, 8), :], 0, 1).astype(F32)

    ring_gather(lambda k, c: held.at[k, c], send_sem, recv_sem, make, lambda *_: None, on_step)

    def forward(i, carry):
        peak, count, cross = carry
        value, target = logits[chunk(i, 16)], targets[chunk(i, 16)]
        return (
            jnp.maximum(peak, jnp.max(value, axis=0)),
            count + jnp.sum(target, axis=0),
            cross + jnp.sum(target * value, axis=0),
        )

    zero = jnp.zeros(shape, F32)
    peak, count, cross = lax.fori_loop(0, 8, forward, (jnp.full(shape, -jnp.inf, F32), zero, zero))
    spread = lax.fori_loop(
        0, 8, lambda i, t: t + jnp.sum(jnp.exp(logits[chunk(i, 16)] - peak[None]), axis=0), zero
    )
    for i, value in enumerate((peak, spread, count, cross)):
        stats[i] = value
    peak, spread, count, cross = merge_stats(stats, merged, got, stat_send, stat_recv, stat_own)
    lse = peak + jnp.log(spread)
    bins = 128 * lax.axis_size("seq")
    loss_ref[...] = (count * lse - cross) / bins

    @pl.loop(0, 8)
    def _(i):
        value = (count[None] * jnp.exp(logits[chunk(i, 16)] - lse[None]) - targets[chunk(i, 16)]) * (1.0 / bins)
        grad_ref[chunk(i, 128), :] = value.reshape(128, shape[1]).astype(BF)


def second_layer(pre_two, hidden_one, head_weight, counts):
    tracks = head_weight.shape[1]
    stat = (4, NZ, tracks)
    return call(
        second_kernel,
        "second_layer",
        2,
        [((ROWS, 192 * NZ), BF), ((ROWS, tracks), BF), ((NZ, tracks), F32)],
        whole(4),
        [
            pltpu.VMEM((NZ, 4, 384, 128), BF),
            pltpu.VMEM((128, NZ, tracks), F32),
            pltpu.VMEM((128, NZ, tracks), F32),
            pltpu.VMEM(stat, F32),
            pltpu.VMEM((2, *stat), F32),
            pltpu.VMEM((3, 4, *stat), F32),
            DMA((2, 4, 4)),
            DMA((2, 4, 4)),
            DMA((3, 3)),
            DMA((3, 3)),
            DMA((3,)),
        ],
        pre_two,
        hidden_one,
        head_weight,
        counts,
    )


def ring_scatter(own, got, sent, send_sem, recv_sem, pair_of, hook):
    z, right, left = z_neighbours()
    piece = lambda h: pl.ds(h * HALF, HALF)
    far = lax.rem(z + 4, NZ) // 2
    pair_of(far)
    copies = {}
    for step in range(4):
        for half in (0, 1):
            for way in (0, 1):
                if step == 0 and half != way:
                    continue
                sign = 1 if way == 0 else -1
                block = lax.rem(z + sign * (4 - step) + NZ, NZ)
                before = copies.get((way, step - 1, half))
                if before is None:
                    source = own.at[block, piece(half)]
                else:
                    before.wait_recv()
                    sent[way, step - 1, piece(half), :] = (
                        got[way, step - 1, piece(half), :].astype(F32) + own[block, piece(half), :].astype(F32)
                    ).astype(BF)
                    source = sent.at[way, step - 1, piece(half)]
                copy = remote(
                    source,
                    got.at[way, step, piece(half)],
                    send_sem.at[way, step, half],
                    recv_sem.at[way, step, half],
                    {"dp": right if way == 0 else left},
                )
                copy.start()
                copies[way, step, half] = copy
        if step == 0:
            for d in (1, 3, 2):
                pair_of(lax.rem(far + d, NZ // 2))
        hook(step)
    for half in (0, 1):
        copies[0, 3, half].wait_recv()
        copies[1, 3, half].wait_recv()
    for copy in copies.values():
        copy.wait_send()


def ring_total(own, got, at, size):
    z = lax.axis_index("dp")
    rows = pl.ds(pl.multiple_of(at, 256), size)
    return own[z, rows, :].astype(F32) + got[0, 3, rows, :].astype(F32) + got[1, 3, rows, :].astype(F32)


def ring_result(own, got, i):
    odd = lax.rem(lax.axis_index("dp"), 2) == 1
    rest = ring_total(own, got, ROWS + 256 * i, 256)
    return [
        (index, natural(odd, ring_total(own, got, 256 * index, 256), rest[:, lanes]))
        for index, lanes in ((i, LO), (i + 2, HI))
    ]


def put_pair(own, pair, i, product):
    one, two = 2 * pair, 2 * pair + 1
    for index, value in zip((i, i + 2), product):
        own[one, chunk(index, 256), :] = value[:, 0:128]
        own[two, chunk(index, 256), :] = value[:, 256:384]
    rows = pl.ds(pl.multiple_of(ROWS + 256 * i, 256), 256)
    low, high = product
    own[one, rows, :] = jnp.concatenate([low[:, 128:192], high[:, 128:192]], axis=1)
    own[two, rows, :] = jnp.concatenate([low[:, 192:256], high[:, 192:256]], axis=1)


class Spread:
    def __init__(self, source, result, first, number, scratch):
        self.source, self.result, self.first, self.number = source, result, first, number
        self.pair, self.both, self.early, self.relayed, self.full, self.mid, self.got_two, self.send, self.recv = scratch
        self.y, self.x, self.core = seq_place()
        self.other, self.along_x, self.along_y = seq_peers()

    def stage(self, which):
        along = self.first if which == 1 else ("y" if self.first == "x" else "x")
        return (self.x, self.along_x) if along == "x" else (self.y, self.along_y)

    def copy(self, source, target, slot, peer):
        made = remote(source, target, self.send.at[self.number, slot], self.recv.at[self.number, slot], {"seq": peer})
        made.start()
        return made

    def begin(self):
        self.exchange = self.copy(self.source(1 - self.core), self.pair, 0, self.other)

    def add_pair(self):
        self.exchange.wait_recv()
        mine = self.source(self.core)

        @pl.loop(0, 16)
        def _(i):
            spot = lax.rem(i, 4) * 4 + i // 4 if self.first == "x" else i
            self.both[spot] = (self.pair[i].astype(F32) + mine[i].astype(F32)).astype(BF)

        place, (right, _, left) = self.stage(1)
        far = lax.rem(place + 2, 4)
        self.one, self.last = lax.rem(place + 1, 4), lax.rem(place + 3, 4)
        self.hop = [
            self.copy(self.both.at[pl.ds(4 * far, 2)], self.early.at[0], 1, right),
            self.copy(self.both.at[pl.ds(4 * far + 2, 2)], self.early.at[1], 2, left),
        ]
        self.near = [
            self.copy(self.both.at[pl.ds(4 * self.one + 2, 2)], self.full.at[0, pl.ds(2, 2)], 3, right),
            self.copy(self.both.at[pl.ds(4 * self.last, 2)], self.full.at[1, pl.ds(0, 2)], 4, left),
        ]

    def relay(self):
        _, (right, _, left) = self.stage(1)
        for way, (block, sub, peer) in enumerate(((self.one, 0, right), (self.last, 2, left))):
            self.hop[way].wait_recv()
            for i in range(2):
                total = self.early[way, i].astype(F32) + self.both[4 * block + sub + i].astype(F32)
                self.relayed[way, i] = total.astype(BF)
            self.near.append(self.copy(self.relayed.at[way], self.full.at[way, pl.ds(sub, 2)], 5 + way, peer))

    def add_first(self):
        for copy in self.near:
            copy.wait_recv()
        place, _ = self.stage(1)

        @pl.loop(0, 4)
        def _(i):
            total = self.both[4 * place + i].astype(F32)
            for way in range(2):
                total = total + self.full[way, i].astype(F32)
            self.mid[i] = total.astype(BF)

        place, peers = self.stage(2)
        self.later = []
        for d, peer in enumerate(peers):
            target = lax.rem(place + d + 1, 4)
            self.later.append(self.copy(self.mid.at[target], self.got_two.at[2 - d], 7 + d, peer))

    def finish(self):
        for copy in self.later:
            copy.wait_recv()
        place, _ = self.stage(2)
        total = self.mid[place].astype(F32)
        for d in range(3):
            total = total + self.got_two[d].astype(F32)
        self.result[...] = total
        for copy in [self.exchange, *self.hop, *self.near, *self.later]:
            copy.wait_send()


SPREAD_REFS = 7


def spread_scratch(rows, width):
    return [
        pltpu.VMEM((16, rows, width), BF),
        pltpu.VMEM((16, rows, width), BF),
        pltpu.VMEM((2, 2, rows, width), BF),
        pltpu.VMEM((2, 2, rows, width), BF),
        pltpu.VMEM((2, 4, rows, width), BF),
        pltpu.VMEM((4, rows, width), BF),
        pltpu.VMEM((3, rows, width), BF),
    ]


def conv_pieces(last_split):
    pieces = [(0, 0, 48, "x"), (1, 0, 48, "y")]
    return pieces + ([(2, 0, 16, "x"), (2, 16, 32, "y")] if last_split else [(2, 0, 48, "x")])


def conv_spreads(grads, result, pieces, refs):
    *refs, send, recv = refs
    made = []
    for number, (tap, row, rows, axis) in enumerate(pieces):
        mine = refs[SPREAD_REFS * number : SPREAD_REFS * (number + 1)]
        made.append(
            Spread(
                lambda core, tap=tap, row=row, rows=rows: grads.at[tap, :, core, pl.ds(row, rows)],
                result.at[tap, pl.ds(row, rows)],
                axis,
                number,
                (*mine, send, recv),
            )
        )
    return made


def conv_spread_scratch(pieces):
    made = [pltpu.VMEM((3, 16, 2, 48, 192), BF)]
    for _, _, rows, _ in pieces:
        made += spread_scratch(rows, 192)
    return made + [DMA((len(pieces), 10)), DMA((len(pieces), 10))]


def ring_scratch():
    return [
        pltpu.VMEM((NZ, *PACKED), BF),
        pltpu.VMEM((2, 4, *PACKED), BF),
        pltpu.VMEM((2, 3, *PACKED), BF),
        DMA((2, 4, 2)),
        DMA((2, 4, 2)),
    ]


def seq_hellos():
    other, along_x, along_y = seq_peers()
    return [other, *along_x, *along_y]


def third_kernel(
    grad_ref,
    head_ref,
    rows_ref,
    pre_ref,
    back_ref,
    up_ref,
    head_out,
    own,
    got,
    sent,
    send_sem,
    recv_sem,
    head_grad,
    *rest,
):
    *scratch, edge_send, edge_recv = rest
    z, right, left = z_neighbours()
    s, after, before = seq_neighbours()
    met = greet_later(
        [{"dp": right}, {"dp": left}, {"seq": after}, {"seq": before}] + [{"seq": p} for p in seq_hellos()]
    )
    started = []

    def pair_of(p):
        @pl.loop(0, 2)
        def _(i):
            product = [
                lax.dot_general(
                    grad_ref[chunk(index, 256), :],
                    head_ref[chunk(p, 384), :],
                    (((1,), (1,)), ((), ())),
                    preferred_element_type=F32,
                ).astype(BF)
                for index in (i, i + 2)
            ]
            put_pair(own, p, i, product)

        if not started:
            met()
            started.append(1)

    spread = Spread(lambda core: head_grad.at[:, core], head_out, "x", 0, scratch)

    def hook(step):
        if step == 0:

            @pl.loop(0, 4)
            def _(c):
                value = lax.dot_general(
                    rows_ref[:, chunk(c, 384)], grad_ref[...], (((0,), (0,)), ((), ())), preferred_element_type=F32
                )
                head_grad[chunk(c, 4)] = value.astype(BF).reshape(4, 2, 48, value.shape[1])

            spread.begin()
        elif step == 1:
            spread.add_pair()
        elif step == 2:
            spread.relay()
        else:
            spread.add_first()

    ring_scatter(own, got, sent, send_sem, recv_sem, pair_of, hook)

    @pl.loop(0, 2)
    def _(i):
        for index, value in ring_result(own, got, i):
            back_ref[chunk(index, 256), :] = value
            up = (value * activate_slope(pre_ref[chunk(index, 256), :])).astype(BF)
            up_ref[pl.ds(DMAX + 32 * index, 32)] = up.reshape(32, NZ, 192)

    edges = []
    for side, (src, dst, peer) in enumerate(((128, 0, after), (DMAX, DMAX + 128, before))):
        copy = remote(
            up_ref.at[pl.ds(src, DMAX)], up_ref.at[pl.ds(dst, DMAX)], edge_send.at[side], edge_recv.at[side], {"seq": peer}
        )
        copy.start()
        edges.append(copy)
    for copy in edges:
        copy.wait_recv()
        copy.wait_send()
    for at, drop in ((0, s == 0), (DMAX + 128, s == lax.axis_size("seq") - 1)):

        @pl.when(drop)
        def _():
            up_ref[at : at + DMAX] = jnp.zeros_like(up_ref[at : at + DMAX])

    spread.finish()


def third_layer(logit_grad, head_weight, head_rows, pre_two):
    tracks = head_weight.shape[1]
    return call(
        third_kernel,
        "third_layer",
        3,
        [((ROWS, 192), F32), ((128 + 2 * DMAX, NZ, 192), BF), ((48, tracks), F32)],
        whole(4),
        ring_scratch()
        + [pltpu.VMEM((16, 2, 48, tracks), BF)]
        + spread_scratch(48, tracks)
        + [DMA((1, 10)), DMA((1, 10)), DMA((2,)), DMA((2,))],
        logit_grad,
        head_weight,
        head_rows,
        pre_two,
    )


def tap_grad(framed, spacing, up, tap, into):
    @pl.loop(0, 4)
    def _(c):
        rows = framed[pl.ds(DMAX + (tap - 1) * spacing, 128), :, chunk(c, 384)].reshape(ROWS, 384)
        value = lax.dot_general(rows, up, (((0,), (0,)), ((), ())), preferred_element_type=F32)
        into[chunk(c, 4)] = value.astype(BF).reshape(4, 2, 48, 192)


def fourth_kernel(
    gaps,
    up_ref,
    w_ref,
    back_ref,
    pre_ref,
    f_ref,
    one_ref,
    two_out,
    own,
    got,
    sent,
    send_sem,
    recv_sem,
    grads,
    *spread_refs,
):
    z, right, left = z_neighbours()
    met = greet_later([{"dp": right}, {"dp": left}] + [{"seq": p} for p in seq_hellos()])
    gap = gaps[1]
    started = []

    def pair_of(p):
        @pl.loop(0, 2)
        def _(i):
            product = []
            for index in (i, i + 2):
                total = None
                for tap in range(3):
                    rows = up_ref[pl.ds(DMAX - (tap - 1) * gap + 32 * index, 32)].reshape(256, 192)
                    term = jnp.dot(rows, w_ref[tap, :, chunk(p, 384)], preferred_element_type=F32)
                    total = term if total is None else total + term
                product.append(total.astype(BF))
            put_pair(own, p, i, product)

        if not started:
            met()
            started.append(1)

    spreads = conv_spreads(grads, two_out, conv_pieces(False), spread_refs)

    def hook(step):
        up = lambda: up_ref[DMAX : DMAX + 128].reshape(ROWS, 192)
        if step == 0:
            tap_grad(f_ref, gap, up(), 0, grads.at[0])
            spreads[0].begin()
        elif step == 1:
            tap_grad(f_ref, gap, up(), 1, grads.at[1])
            spreads[1].begin()
            tap_grad(f_ref, gap, up(), 2, grads.at[2])
            spreads[2].begin()
        elif step == 2:
            for t in range(3):
                spreads[t].add_pair()
        else:
            for spread in spreads:
                spread.relay()

    ring_scatter(own, got, sent, send_sem, recv_sem, pair_of, hook)
    for spread in spreads:
        spread.add_first()

    @pl.loop(0, 2)
    def _(i):
        for index, value in ring_result(own, got, i):
            rows = chunk(index, 256)
            one_ref[rows, :] = ((back_ref[rows, :] + value) * activate_slope(pre_ref[rows, :])).astype(BF)

    for t in range(3):
        spreads[t].finish()


def fourth_layer(gaps, framed_up, weight, back, pre_one, framed_one):
    return call(
        fourth_kernel,
        "fourth_layer",
        4,
        [((ROWS, 192), BF), ((3, 48, 192), F32)],
        [SMEM] + whole(5),
        ring_scratch() + conv_spread_scratch(conv_pieces(False)),
        gaps,
        framed_up,
        weight,
        back,
        pre_one,
        framed_one,
    )


def fifth_kernel(gaps, fe_ref, up_ref, one_out, grads, *spread_refs):
    met = greet_later([{"seq": p} for p in seq_hellos()])
    pieces = conv_pieces(True)
    spreads = conv_spreads(grads, one_out, pieces, spread_refs)
    for tap in range(3):
        tap_grad(fe_ref, gaps[0], up_ref[...], tap, grads.at[tap])
        if tap == 0:
            met()
        for piece, spread in zip(pieces, spreads):
            if piece[0] == tap:
                spread.begin()
        if tap == 2:
            spreads[0].add_pair()
    for spread in spreads[1:]:
        spread.add_pair()
    for act in ("relay", "add_first", "finish"):
        for spread in spreads:
            getattr(spread, act)()


def fifth_layer(gaps, framed_in, up_one):
    return call(
        fifth_kernel,
        "fifth_layer",
        5,
        [((3, 48, 192), F32)],
        [SMEM] + whole(2),
        conv_spread_scratch(conv_pieces(True)),
        gaps,
        framed_in,
        up_one,
    )[0]


def on_device(embeddings, conv_one, conv_two, head_weight, counts, dilation):
    framed_in, pre_one, hidden_one, framed_one, pre_two = first_layer(dilation, embeddings[0], conv_one, conv_two)
    head_rows, logit_grad, track_loss = second_layer(pre_two, hidden_one, head_weight, counts)
    grad_two_out, framed_up, grad_head = third_layer(logit_grad, head_weight, head_rows, pre_two)
    up_one, grad_two = fourth_layer(dilation, framed_up, conv_two, grad_two_out, pre_one, framed_one)
    grad_one = fifth_layer(dilation, framed_in, up_one)
    return (track_loss, grad_head, grad_one, grad_two)


def solution(mesh):
    placed = (
        P("dp", "seq", None),
        P(None, "dp", None),
        P(None, "dp", None),
        P(None, "dp"),
        P(None, "seq", "dp"),
        P(),
    )
    return jax.shard_map(
        on_device,
        mesh=mesh,
        in_specs=placed,
        out_specs=(P(None, "dp"), P("seq", "dp"), P(None, "seq", "dp"), P(None, "seq", "dp")),
        check_vma=False,
    )
```
